256 devices in a mesh: dp: 32 (over z, x), expert: 8 (over y, core).
Axes of the slice: x: 4, y: 4, z: 8, core: 2. Of those that a mesh axis runs over, the one named last changes fastest.
Arguments:
- grads: bfloat16 [32, 8, 2048, 1024], P('dp', 'expert'), may hold values from -100 to 100
- signs: int32 [8, 1024], P('expert'), may hold values from -1 to 1, as said below
- weights: bfloat16 [8, 2048, 1024], P('expert', 'dp'), may hold values from -4 to 4
- compensation: bfloat16 [8, 2048, 1024], P('expert', 'dp'), may hold values from -0.099609375 to 0.099609375
Outputs:
- new_weights: bfloat16 [8, 2048, 1024], P('expert')
- update_grad: float32 [8, 2048, 1024], P('expert', 'dp')
The draws below stay inside these ranges and needn't reach their ends.
Inputs may be any that keep to these rules, and one draw needn't show every extreme that they name: `signs`: each entry is -1 or +1.
All inputs are finite; a program needn't handle non-finite values.
Results may differ from the reference program's by a relative error of at most 0.0018.
The reference program's roundings to bfloat16 on the way (of `quant`) count: a program that leaves them out, or rounds other values in their place, can miss the bound.
Values may be sent and summed in bfloat16 or wider, within the bound.
A program may use at most 64 MiB of HBM per device.

```python
import math
import jax
import jax.numpy as jnp
from jax import lax

HBLOCK = 1024
REPLICAS = 32
EXPERTS = 8
BLOCKS = 2048


def draw_grads(key, part):
    first, second = jax.random.split(key, 2)
    shape = (REPLICAS, EXPERTS, BLOCKS, HBLOCK)
    noise = jnp.clip(jax.random.normal(first, shape, jnp.float32), -6.0, 6.0)
    steps = jnp.arange(REPLICAS, dtype=jnp.float32) / max(REPLICAS - 1, 1)
    rising = jnp.exp(steps * math.log(3.0))
    factor = jnp.exp(jax.random.uniform(second, (REPLICAS, EXPERTS, BLOCKS, 1), jnp.float32, math.log(0.5), math.log(5.0)))
    return (noise * rising[:, None, None, None] * factor).astype(jnp.bfloat16)


def draw_signs(key, part):
    picks = jax.random.randint(jax.random.fold_in(key, 7), (EXPERTS, HBLOCK), 0, 2)
    return (2 * picks - 1).astype(jnp.int32)


def level_of(stream_key, extent, shards, low, top_value):
    def one(dim, shards_of):
        steps = jax.random.uniform(jax.random.fold_in(jax.random.fold_in(stream_key, 6), dim), (shards_of,), jnp.float32, low / len(shards), top_value / len(shards))
        return jnp.repeat(jnp.exp(steps), extent[dim] // shards_of).reshape((-1,) + (1,) * (len(extent) - dim - 1))

    gain = one(*shards[0])
    for cut in shards[1:]:
        gain = gain * one(*cut)
    return gain


def bell_draw(rng, extent, spread, reach, cuts=(), kind=jnp.bfloat16):
    values = spread * jax.random.normal(rng, extent, jnp.float32)
    if cuts:
        values = values * level_of(rng, extent, cuts, -0.22, 0.18)
    return jnp.clip(values, -reach, reach).astype(kind)


def setup_inputs(seed: int = 0) -> dict:
    key_of = jax.random.split(jax.random.key(seed), 5)
    return {
        "grads": draw_grads(jax.random.fold_in(key_of[4], 71), 0),
        "signs": draw_signs(jax.random.fold_in(key_of[4], 71), 0),
        "weights": bell_draw(key_of[2], (EXPERTS, BLOCKS, HBLOCK), 1.0, 4.0, ((0, 8), (1, 32))),
        "compensation": jnp.clip(jax.random.uniform(key_of[3], (EXPERTS, BLOCKS, HBLOCK), jnp.float32, -0.099609375, 0.099609375) * level_of(key_of[3], (EXPERTS, BLOCKS, HBLOCK), ((0, 8), (1, 32)), -0.4, 0.0), -0.099609375, 0.099609375).astype(jnp.bfloat16),
    }


clamp_level = 2.0
target_rms = 0.2
learn_rate = 0.02

def walsh(values):
    width = values.shape[-1]
    lead = values.shape[:-1]
    half = 1
    while half < width:
        pairs = values.reshape(lead + (width // (2 * half), 2, half))
        upper = pairs[..., 0, :]
        lower = pairs[..., 1, :]
        values = jnp.stack([upper + lower, upper - lower], axis=-2).reshape(lead + (width,))
        half = half * 2
    return values

def reference(grads, signs, weights, compensation):
    inverse_root = 1.0 / math.sqrt(HBLOCK)
    sign_rows = signs.astype(jnp.float32)

    def per_expert(inputs):
        expert_grads, sign_row = inputs
        rotated = walsh(expert_grads.astype(jnp.float32) * sign_row) * inverse_root
        rms = jnp.sqrt(lax.optimization_barrier(jnp.mean(rotated * rotated, axis=-1)) + 1e-06)
        scale = lax.optimization_barrier(jnp.max(rms, axis=0))
        quant = jnp.clip(rotated / scale[None, :, None], -clamp_level, clamp_level).astype(jnp.bfloat16)
        quant = lax.optimization_barrier(quant)
        total = lax.optimization_barrier(jnp.sum(quant.astype(jnp.float32), axis=0))
        mean_rot = total * scale[:, None] / REPLICAS
        return walsh(mean_rot) * inverse_root * sign_row
    unrot = lax.map(per_expert, (jnp.transpose(grads, (1, 0, 2, 3)), sign_rows))
    squares = jnp.sum(unrot * unrot)
    limit = target_rms * math.sqrt(EXPERTS * BLOCKS * HBLOCK)
    factor = limit / jnp.maximum(jnp.sqrt(squares), limit)
    update_grad = unrot * factor
    summed = weights.astype(jnp.float32) + (compensation.astype(jnp.float32) - learn_rate * update_grad)
    new_weights = summed.astype(jnp.bfloat16)
    return (new_weights, update_grad)
```

```python
import heapq
import math

import jax
import jax.numpy as jnp
from jax import lax
from jax.experimental import pallas as pl
from jax.experimental.pallas import tpu as pltpu
from jax.sharding import PartitionSpec as P

MESH = pl.DeviceIdType.MESH
F32 = jnp.float32
BF16 = jnp.bfloat16

clamp_level = 2.0
target_rms = 0.2
learn_rate = 0.02

Z, X, Y, CORES = 8, 4, 4, 2
ROWS, WIDTH, OWNED = 2048, 1024, 64
GROUP = ROWS // Z
SUB = 256
HALF = OWNED // 2
TILE = 16
R1 = 24
ORDER = (4, 3, -3, 2, -2, 1, -1, 0)
NX, NZ, NE = X - 1, Z - 1, Y * CORES - 1


def gather_plan():
    copies = {}

    def add(name, link, lo, hi, after, block):
        copies[name] = dict(link=link, lo=lo, hi=hi, after=after, block=block)

    def z_chain(tag, dx, lo, hi, cut, after):
        for sign, link in ((1, "z+"), (-1, "z-")):
            prev = after
            for k in range(4):
                a, b = lo, hi
                if k == 3:
                    a, b = (lo, cut) if sign == 1 else (cut, hi)
                if b > a:
                    add((tag, link, k), link, a, b, prev, (-sign * (k + 1), dx))
                prev = ((tag, link, k),)

    def x_step(tag, dz, lo, hi, cut, after):
        for sign, link in ((1, "x+"), (-1, "x-")):
            add((tag, link, 0), link, lo, hi, after, (dz, -sign))
            a, b = (lo, cut) if sign == 1 else (cut, hi)
            add((tag, link, 1), link, a, b, ((tag, link, 0),), (dz, -2 * sign))

    x_step("p1x", 0, 0, R1, 16, ())
    z_chain("p2z", 0, R1, OWNED, R1 + 24, ())
    x_step("p2x0", 0, R1, OWNED, R1 + 24, ())
    z_chain("p1z0", 0, 0, R1, 8, ())
    z_chain("p1z1", -1, 0, R1, 8, (("p1x", "x+", 0),))
    z_chain("p1z-1", 1, 0, R1, 8, (("p1x", "x-", 0),))
    z_chain("p1z2", 2, 0, R1, 8, (("p1x", "x+", 1), ("p1x", "x-", 1)))
    for k in range(4):
        cut = R1 + (16 if k % 2 else 24)
        if k < 3:
            x_step(f"p2x{k + 1}", -(k + 1), R1, OWNED, cut, (("p2z", "z+", k),))
            x_step(f"p2x{-k - 1}", k + 1, R1, OWNED, OWNED + R1 - cut, (("p2z", "z-", k),))
        else:
            x_step("p2x4", 4, R1, OWNED, cut, (("p2z", "z+", 3), ("p2z", "z-", 3)))

    per_row, hop = WIDTH * 2 / 45e3, 1.7
    free = {link: 0.0 for link in ("x+", "x-", "z+", "z-")}
    events, done, order = [], set(), []
    started = set()

    def start_ready(now, current):
        names = []
        for name, c in copies.items():
            if name not in started and all(a in done for a in c["after"]):
                started.add(name)
                begin = max(now, free[c["link"]])
                end = begin + (c["hi"] - c["lo"]) * per_row
                free[c["link"]] = end
                heapq.heappush(events, (end + hop, len(started), name))
                names.append(name)
        order.append((current, names))

    start_ready(0.0, None)
    last = 0.0
    while events:
        last, _, name = heapq.heappop(events)
        done.add(name)
        start_ready(last, name)
    return copies, order, last


def kernel_body(
    grads, signs, weights, comp, out, upd,
    gbuf, rot, quant, left_in, right_in, far_in, left_relay, right_relay,
    zsend, zrecv, total, hmat,
    cbuf, cx, cz, sbuf, se, sx, sz,
    load_sem, small_send, small_recv, rs_send, rs_recv, zring_send, zring_recv, ag_send, ag_recv,
):
    dp = lax.axis_index("dp")
    expert = lax.axis_index("expert")
    z, x = dp // X, lax.rem(dp, X)
    inverse_root = 1.0 / math.sqrt(WIDTH)

    def at(dz, dx, de=0):
        other_z = lax.rem(z + (dz + Z), Z)
        other_x = lax.rem(x + (dx + X), X)
        other_e = lax.rem(expert + de, Y * CORES) if de else expert
        return (other_z * X + other_x, other_e)

    def remote(src, dst, send, recv, where):
        return pltpu.make_async_remote_copy(
            src_ref=src, dst_ref=dst, send_sem=send, recv_sem=recv,
            device_id=where, device_id_type=MESH,
        )

    pending = []

    def send(src, dst, ssem, rsem, where):
        copy = remote(src, dst, ssem, rsem, where)
        copy.start()
        pending.append(copy)

    def wait_for(dst, ssem, rsem):
        remote(dst, dst, ssem, rsem, at(0, 1)).wait_recv()

    barrier = pltpu.get_barrier_semaphore()
    peers = [at(0, d) for d in range(1, X)]
    peers += [at(d, 0) for d in range(1, Z)]
    peers += [at(0, 0, d) for d in range(1, Y * CORES)]
    for peer in peers:
        pl.semaphore_signal(barrier, inc=1, device_id=peer, device_id_type=MESH)

    loads = []
    for g in range(Z):
        rows = pl.ds(g * GROUP, GROUP)
        copy = pltpu.make_async_copy(grads.at[rows, :], gbuf.at[rows, :], load_sem.at[g])
        copy.start()
        loads.append(copy)

    common = lax.broadcasted_iota(jnp.int32, (SUB, SUB), 0) & lax.broadcasted_iota(
        jnp.int32, (SUB, SUB), 1
    )
    for shift in (4, 2, 1):
        common = common ^ (common >> shift)
    plain = (1 - 2 * (common & 1)).astype(F32)
    hmat[4] = plain.astype(BF16)
    sign_row = signs[...].astype(F32)
    for a in range(4):
        hmat[a] = (plain * sign_row[:, a * SUB : (a + 1) * SUB]).astype(BF16)

    lane = lax.broadcasted_iota(jnp.int32, (TILE, 128), 1)

    squares = jnp.zeros((TILE, 128), F32)
    for g in range(Z):
        loads[g].wait()

        def measure(i, acc, g=g):
            tile = gbuf[pl.ds(pl.multiple_of(g * GROUP + i * TILE, TILE), TILE), :].astype(F32)
            tile = tile * tile
            part = tile[:, 0:128]
            for a in range(1, WIDTH // 128):
                part = part + tile[:, a * 128 : (a + 1) * 128]
            row = jnp.sum(part, axis=1, keepdims=True)
            return jnp.where(lane == g * (GROUP // TILE) + i, row, acc)

        squares = lax.fori_loop(0, GROUP // TILE, measure, squares, unroll=4)
    cbuf[0] = squares

    pl.semaphore_wait(barrier, len(peers))

    def rotate(g, _):
        rows = pl.ds(pl.multiple_of(g * GROUP, GROUP), GROUP)
        for a in range(4):
            cols = slice(a * SUB, (a + 1) * SUB)
            rot[rows, cols] = lax.dot_general(
                gbuf[rows, cols], hmat[a], (((1,), (1,)), ((), ())), preferred_element_type=F32
            )
        return 0

    for d in range(1, X):
        send(cbuf.at[0], cx.at[d - 1], small_send.at[d - 1], small_recv.at[d - 1], at(0, d))
    lax.fori_loop(0, 3, rotate, 0)
    best = cbuf[0]
    for d in range(1, X):
        wait_for(cx.at[d - 1], small_send.at[d - 1], small_recv.at[d - 1])
        best = jnp.maximum(best, cx[d - 1])
    cbuf[1] = best
    for d in range(1, Z):
        k = NX + d - 1
        send(cbuf.at[1], cz.at[d - 1], small_send.at[k], small_recv.at[k], at(d, 0))
    lax.fori_loop(3, Z, rotate, 0)
    for d in range(1, Z):
        k = NX + d - 1
        wait_for(cz.at[d - 1], small_send.at[k], small_recv.at[k])
        best = jnp.maximum(best, cz[d - 1])
    scale = jnp.sqrt(best * (1.0 / WIDTH) + 1e-06)
    cbuf[2] = scale
    cbuf[3] = inverse_root / scale

    def row_values(index, which):
        return jnp.sum(jnp.where(lane == index, cbuf[which], 0.0), axis=1, keepdims=True)

    def butterfly(parts):
        u0, u1 = parts[0] + parts[1], parts[0] - parts[1]
        u2, u3 = parts[2] + parts[3], parts[2] - parts[3]
        return u0 + u2, u1 + u3, u0 - u2, u1 - u3

    def quantize(zt):
        def step(i, _):
            index = zt * (GROUP // TILE) + i
            rows = pl.ds(pl.multiple_of(index * TILE, TILE), TILE)
            inverse = row_values(index, 3)
            parts = [rot[rows, a * SUB : (a + 1) * SUB] for a in range(4)]
            for a, part in enumerate(butterfly(parts)):
                level = jnp.clip(part * inverse, -clamp_level, clamp_level)
                quant[rows, a * SUB : (a + 1) * SUB] = level.astype(BF16)
            return 0

        lax.fori_loop(0, GROUP // TILE, step, 0, unroll=2)

    def owner_z(d):
        return lax.rem(z + (d + Z), Z)

    def quant_rows(zt, dx, lo, n):
        first = zt * GROUP + lax.rem(x + (dx + X), X) * OWNED + lo
        return quant.at[pl.ds(pl.multiple_of(first, TILE), n), :]

    def send_group(i):
        zt = owner_z(ORDER[i])
        quantize(zt)
        s, r = rs_send.at[i], rs_recv.at[i]
        send(quant_rows(zt, 2, 0, HALF), left_relay.at[i], s.at[0], r.at[0], at(0, 1))
        send(quant_rows(zt, 2, HALF, HALF), right_relay.at[i], s.at[1], r.at[1], at(0, -1))
        send(quant_rows(zt, 1, 0, OWNED), left_in.at[i], s.at[2], r.at[2], at(0, 1))
        send(quant_rows(zt, -1, 0, OWNED), right_in.at[i], s.at[3], r.at[3], at(0, -1))

    def relay_group(i):
        s, r = rs_send.at[i], rs_recv.at[i]
        low, high = pl.ds(0, HALF), pl.ds(HALF, HALF)
        wait_for(left_relay.at[i], s.at[0], r.at[0])
        send(left_relay.at[i], far_in.at[i, low, :], s.at[4], r.at[4], at(0, 1))
        wait_for(right_relay.at[i], s.at[1], r.at[1])
        send(right_relay.at[i], far_in.at[i, high, :], s.at[5], r.at[5], at(0, -1))

    def zsem(kind, dirn, d):
        return kind.at[dirn, d]

    def sum_group(i):
        d = ORDER[i]
        zt = owner_z(d)
        s, r = rs_send.at[i], rs_recv.at[i]
        low, high = pl.ds(0, HALF), pl.ds(HALF, HALF)
        wait_for(left_in.at[i], s.at[2], r.at[2])
        wait_for(right_in.at[i], s.at[3], r.at[3])
        wait_for(far_in.at[i, low, :], s.at[4], r.at[4])
        wait_for(far_in.at[i, high, :], s.at[5], r.at[5])
        base = zt * GROUP + x * OWNED

        def here(t):
            rows = pl.ds(pl.multiple_of(t * TILE, TILE), TILE)
            own = quant[pl.ds(pl.multiple_of(base + t * TILE, TILE), TILE), :].astype(F32)
            near = left_in[i, rows, :].astype(F32) + right_in[i, rows, :].astype(F32)
            return rows, own + near + far_in[i, rows, :].astype(F32)

        def run(lo, hi, dst, extra):
            def step(t, _):
                rows, value = here(t)
                for ref in extra:
                    value = value + ref[rows, :]
                dst[rows, :] = value
                return 0

            lax.fori_loop(lo // TILE, hi // TILE, step, 0)

        def pass_on(dirn, d, rows):
            k = d - 1
            send(
                zsend.at[dirn, k, rows, :], zrecv.at[dirn, k, rows, :],
                zring_send.at[dirn, k], zring_recv.at[dirn, k], at(1 if dirn == 0 else -1, 0),
            )

        def arrived(dirn, k, rows):
            wait_for(zrecv.at[dirn, k, rows, :], zring_send.at[dirn, k], zring_recv.at[dirn, k])

        every = pl.ds(0, OWNED)
        if d == 4:
            run(0, HALF, zsend.at[0, 3], ())
            run(HALF, OWNED, zsend.at[1, 3], ())
            pass_on(0, 4, low)
            pass_on(1, 4, high)
        elif d == 0:
            arrived(0, 0, every)
            arrived(1, 0, every)
            run(0, OWNED, total, (zrecv.at[0, 0], zrecv.at[1, 0]))
        else:
            dirn, k = (0, d) if d > 0 else (1, -d)
            slot, kept = zsend.at[dirn, k - 1], zrecv.at[dirn, k]
            if k == 3:
                arrived(dirn, 3, low if dirn == 0 else high)
                run(0, HALF, slot, (kept,) if dirn == 0 else ())
                run(HALF, OWNED, slot, (kept,) if dirn == 1 else ())
            else:
                arrived(dirn, k, every)
                run(0, OWNED, slot, (kept,))
            pass_on(dirn, k, every)

    for step in range(Z + 2):
        if step < Z:
            send_group(step)
        if 1 <= step <= Z:
            relay_group(step - 1)
        if step >= 2:
            sum_group(step - 2)

    def scale_rows(t, acc):
        rows = pl.ds(pl.multiple_of(t * TILE, TILE), TILE)
        mean = total[rows, :] * row_values(dp * (OWNED // TILE) + t, 2) * (1.0 / (Z * X))
        total[rows, :] = mean
        mean = mean * mean
        part = mean[:, 0:128]
        for a in range(1, WIDTH // 128):
            part = part + mean[:, a * 128 : (a + 1) * 128]
        return acc + part[0:8] + part[8:16]

    sbuf[0] = lax.fori_loop(0, OWNED // TILE, scale_rows, jnp.zeros((8, 128), F32))
    first = NX + NZ
    for d in range(1, NE + 1):
        k = first + d - 1
        send(sbuf.at[0], se.at[d - 1], small_send.at[k], small_recv.at[k], at(0, 0, d))

    parts = butterfly([total[:, a * SUB : (a + 1) * SUB] for a in range(4)])
    for a, part in enumerate(parts):
        high = part.astype(BF16)
        rest = part - high.astype(F32)
        middle = rest.astype(BF16)
        low = (rest - middle.astype(F32)).astype(BF16)
        value = jnp.dot(low, hmat[4], preferred_element_type=F32)
        value = value + jnp.dot(middle, hmat[4], preferred_element_type=F32)
        value = value + jnp.dot(high, hmat[4], preferred_element_type=F32)
        cols = slice(a * SUB, (a + 1) * SUB)
        upd[:, cols] = value * (sign_row[:, cols] * inverse_root)

    def reduce_over(source, slots, count, base, dst):
        value = sbuf[source]
        for d in range(1, count + 1):
            k = base + d - 1
            wait_for(slots.at[d - 1], small_send.at[k], small_recv.at[k])
            value = value + slots[d - 1]
        if dst is not None:
            sbuf[dst] = value
        return value

    reduce_over(0, se, NE, first, 1)
    first += NE
    for d in range(1, X):
        k = first + d - 1
        send(sbuf.at[1], sx.at[d - 1], small_send.at[k], small_recv.at[k], at(0, d))
    reduce_over(1, sx, NX, first, 2)
    first += NX
    for d in range(1, Z):
        k = first + d - 1
        send(sbuf.at[2], sz.at[d - 1], small_send.at[k], small_recv.at[k], at(d, 0))
    vector = reduce_over(2, sz, NZ, first, None)
    sum_squares = jnp.sum(jnp.sum(vector, axis=1, keepdims=True), axis=0, keepdims=True)
    limit = target_rms * math.sqrt(ROWS * WIDTH * Y * CORES)
    factor = limit / jnp.maximum(jnp.sqrt(sum_squares), limit)

    def update(t, _):
        rows = pl.ds(pl.multiple_of(t * TILE, TILE), TILE)
        grad = upd[rows, :] * factor
        upd[rows, :] = grad
        new = weights[rows, :].astype(F32) + (comp[rows, :].astype(F32) - learn_rate * grad)
        out[z, x, rows, :] = new.astype(BF16)
        return 0

    lax.fori_loop(0, OWNED // TILE, update, 0)

    copies, order, _ = gather_plan()
    number = {name: k for k, name in enumerate(copies)}
    steps = {"z+": (1, 0), "z-": (-1, 0), "x+": (0, 1), "x-": (0, -1)}

    def view(dz, dx, c):
        rows = pl.ds(c["lo"], c["hi"] - c["lo"])
        other_x = lax.rem(x + (dx + X), X)
        return out.at[lax.rem(z + (dz + Z), Z), other_x, rows, :]

    for arrival, names in order:
        if arrival is not None:
            c, k = copies[arrival], number[arrival]
            wait_for(view(*c["block"], c), ag_send.at[k], ag_recv.at[k])
        for name in names:
            c, k = copies[name], number[name]
            dz, dx = steps[c["link"]]
            block = view(c["block"][0] + dz, c["block"][1] + dx, c)
            send(block, block, ag_send.at[k], ag_recv.at[k], at(dz, dx))

    for copy in pending:
        copy.wait_send()


def on_device(grads, signs, weights, comp):
    copies, _, _ = gather_plan()
    vmem = pl.BlockSpec(memory_space=pltpu.VMEM)
    small = NX + NZ + NE + NX + NZ
    dma = pltpu.SemaphoreType.DMA
    out, upd = pl.pallas_call(
        kernel_body,
        out_shape=(
            pltpu.VMEM((Z, X, OWNED, WIDTH), BF16),
            pltpu.VMEM((OWNED, WIDTH), F32),
        ),
        in_specs=[pl.BlockSpec(memory_space=pl.ANY), vmem, vmem, vmem],
        out_specs=(vmem, vmem),
        scratch_shapes=[
            pltpu.VMEM((ROWS, WIDTH), BF16),
            pltpu.VMEM((ROWS, WIDTH), F32),
            pltpu.VMEM((ROWS, WIDTH), BF16),
            pltpu.VMEM((Z, OWNED, WIDTH), BF16),
            pltpu.VMEM((Z, OWNED, WIDTH), BF16),
            pltpu.VMEM((Z, OWNED, WIDTH), BF16),
            pltpu.VMEM((Z, HALF, WIDTH), BF16),
            pltpu.VMEM((Z, HALF, WIDTH), BF16),
            pltpu.VMEM((2, 4, OWNED, WIDTH), F32),
            pltpu.VMEM((2, 4, OWNED, WIDTH), F32),
            pltpu.VMEM((OWNED, WIDTH), F32),
            pltpu.VMEM((5, SUB, SUB), BF16),
            pltpu.VMEM((4, TILE, 128), F32),
            pltpu.VMEM((NX, TILE, 128), F32),
            pltpu.VMEM((NZ, TILE, 128), F32),
            pltpu.VMEM((3, 8, 128), F32),
            pltpu.VMEM((NE, 8, 128), F32),
            pltpu.VMEM((NX, 8, 128), F32),
            pltpu.VMEM((NZ, 8, 128), F32),
            dma((Z,)),
            dma((small,)),
            dma((small,)),
            dma((Z, 6)),
            dma((Z, 6)),
            dma((2, 4)),
            dma((2, 4)),
            dma((len(copies),)),
            dma((len(copies),)),
        ],
        compiler_params=pltpu.CompilerParams(
            collective_id=0, has_side_effects=True, vmem_limit_bytes=48 * 1024 * 1024
        ),
    )(
        grads.reshape(ROWS, WIDTH),
        signs.reshape(1, WIDTH),
        weights.reshape(OWNED, WIDTH),
        comp.reshape(OWNED, WIDTH),
    )
    return out.reshape(1, ROWS, WIDTH), upd.reshape(1, OWNED, WIDTH)


def solution(mesh):
    in_specs = (
        P("dp", "expert", None, None),
        P("expert", None),
        P("expert", "dp", None),
        P("expert", "dp", None),
    )
    out_specs = (P("expert", None, None), P("expert", "dp", None))
    return jax.shard_map(
        on_device, mesh=mesh, in_specs=in_specs, out_specs=out_specs, check_vma=False
    )
```
